768 devices in a mesh: dp: 16 (over x, z_lo), ctx: 48 (over y, z_hi, core).
Axes of the slice: x: 4, y: 8, z: 12 (z_hi: 3, z_lo: 4; z = z_hi * 4 + z_lo), core: 2. Of those that a mesh axis runs over, the one named last changes fastest.
Arguments:
- query_rows: bfloat16 [16, 6144, 2048], P('dp', 'ctx'), may hold values from -6 to 6
- key_rows: bfloat16 [16, 6144, 512], P('dp', 'ctx'), may hold values from -6 to 6
- value_rows: bfloat16 [16, 6144, 512], P('dp', 'ctx'), may hold values from -6 to 6
- out_grad: bfloat16 [16, 6144, 2048], P('dp', 'ctx'), may hold values from -6 to 6
- segment_ids: int32 [16, 6144], P('dp', 'ctx'), may hold values from 0 to 47, never falling along the last dimension, each value on 1 to 256 neighbouring positions
- home_rows: int32 [16, 768], P('dp', 'ctx'), may hold values from 0 to 15, as said below
Outputs:
- routed: bfloat16 [16, 48, 16, 2, 8, 2048], P('dp', 'ctx')
- query_grad: bfloat16 [16, 6144, 2048], P('dp', 'ctx')
- key_grad: bfloat16 [16, 6144, 512], P('dp', 'ctx')
- value_grad: bfloat16 [16, 6144, 512], P('dp', 'ctx')
The draws below stay inside these ranges and needn't reach their ends.
Inputs may be any that keep to these rules, and one draw needn't show every extreme that they name: `segment_ids`: ids never fall along a sequence; every document holds 1 to 256 tokens, and some document holds exactly 256. `home_rows`: among the 16 stretches of one block, at most 2 name the same dp row; in every block column some dp row is named by exactly 2 stretches of every dp row's block.
All inputs are finite; a program needn't handle non-finite values.
Results may differ from the reference program's by a relative error of at most 0.014.
Values may be sent and summed in bfloat16 or wider, within the bound.
A program may use at most 32 MiB of HBM per device.

```python
import math
import jax
import jax.numpy as jnp
import numpy as np
from jax import lax

HEAD_DIM = 128
QHEADS = 16
KVHEADS = 4
BLOCK_TOK = 128
SPAN = 2
STRETCH = 8
GROUP = 4
STRETCHES = 16
SEQS = 16
BLOCKS = 48
LENGTH = 6144
MAXDOC = 256
DOCS = 48
CAPACITY = 2


def draw_query_rows(key, part):
    width = QHEADS * HEAD_DIM
    field = jnp.clip(jax.random.normal(jax.random.fold_in(key, 21), (SEQS, LENGTH, width)), -6.0, 6.0)
    return field.astype(jnp.bfloat16)


def draw_key_rows(key, part):
    width = KVHEADS * HEAD_DIM
    field = jnp.clip(jax.random.normal(jax.random.fold_in(key, 31), (SEQS, LENGTH, width)), -6.0, 6.0)
    return field.astype(jnp.bfloat16)


def draw_home_rows(key, part):
    full_rows = jax.random.randint(jax.random.fold_in(key, 12), (BLOCKS,), 0, SEQS).astype(jnp.int32)
    block_keys = jax.random.split(jax.random.fold_in(key, 11), SEQS * BLOCKS)
    targets = jnp.tile(full_rows, SEQS)

    def one_block(sub_key, target):
        key_one, key_two = jax.random.split(sub_key)
        spread = (target + 1 + jnp.arange((SEQS - 1) * CAPACITY, dtype=jnp.int32) // CAPACITY) % SEQS
        chosen = jax.random.permutation(key_one, spread)[:STRETCHES - CAPACITY]
        filled = jnp.concatenate([target + jnp.zeros((CAPACITY,), jnp.int32), chosen.astype(jnp.int32)])
        return jax.random.permutation(key_two, filled)
    return jax.vmap(one_block)(block_keys, targets).reshape(SEQS, BLOCKS * STRETCHES).astype(jnp.int32)


def block_levels(stream_key, shape, cuts, low, largest):
    gain = 1.0
    for position, parts in cuts:
        draws = jax.random.uniform(jax.random.fold_in(jax.random.fold_in(stream_key, 6), position), (parts,), jnp.float32, low / len(cuts), largest / len(cuts))
        gain = gain * jnp.repeat(jnp.exp(draws), shape[position] // parts).reshape((-1,) + (1,) * (len(shape) - 1 - position))
    return gain


def split_up(count, total, bound, slope):
    portions = [(1 << 20) // math.isqrt(standing ** slope) + 1 for standing in range(2, count + 1)]
    surplus, counts = total - bound - (count - 1), [1] * (count - 1)
    while surplus > 0:
        free = [i for i in range(count - 1) if counts[i] < bound]
        pool, remaining = sum([portions[i] for i in free]), surplus
        for i in free:
            extra = min(bound - counts[i], max(1, remaining * portions[i] // pool), surplus)
            counts[i] = counts[i] + extra
            surplus = surplus - extra
    return np.array([bound] + counts)


def uneven_parts(rng, count, total, bound, lean):
    if count == 2:
        one = jax.random.randint(rng, (), max(1, total - bound), min(bound, total - 1) + 1)
        return jnp.stack([one, total - one])
    tallies = jnp.asarray(split_up(count, total, bound, lean), jnp.int32)
    twos = (count - 1) // 2
    donor, sink = tallies[1:1 + 2 * twos:2], tallies[2:2 + 2 * twos:2]
    slack = jnp.minimum(donor - 1, bound - sink)
    moved = jax.random.randint(jax.random.fold_in(rng, 1), (twos,), 0, 1 << 20) % (slack + 1)
    tallies = tallies.at[1:1 + 2 * twos:2].set(donor - moved).at[2:2 + 2 * twos:2].set(sink + moved)
    return tallies[jax.random.permutation(jax.random.fold_in(rng, 2), count)]


def noise(own_key, extent, scale, limit, pieces=(), kind=jnp.bfloat16):
    values = jax.random.normal(own_key, extent, jnp.float32) * scale
    if len(pieces) > 0:
        values = block_levels(own_key, extent, pieces, -0.22, 0.18) * values
    return jnp.clip(values, min=-limit, max=limit).astype(kind)


def setup_inputs(seed: int = 0) -> dict:
    key_list = jax.random.split(jax.random.key(seed), 7)
    return {
        "query_rows": draw_query_rows(jax.random.fold_in(key_list[6], 71), 0),
        "key_rows": draw_key_rows(jax.random.fold_in(key_list[6], 71), 0),
        "value_rows": noise(key_list[2], (SEQS, LENGTH, KVHEADS * HEAD_DIM), 1.0, 6.0, ((0, 16), (1, 48))),
        "out_grad": noise(key_list[3], (SEQS, LENGTH, QHEADS * HEAD_DIM), 1.0, 6.0, ((0, 16), (1, 48))),
        "segment_ids": jax.vmap(lambda own: jnp.searchsorted(jnp.cumsum(uneven_parts(own, DOCS, LENGTH, MAXDOC, 2)), jnp.arange(LENGTH), side="right"))(jax.random.split(key_list[4], SEQS)).reshape((SEQS, LENGTH)).astype(jnp.int32),
        "home_rows": draw_home_rows(jax.random.fold_in(key_list[6], 71), 0),
    }


def block_terms(query_block, key_window, value_window, grad_block, allowed):
    scaling = 1.0 / math.sqrt(HEAD_DIM)
    window = key_window.shape[0]
    query_heads = query_block.astype(jnp.float32).reshape(BLOCK_TOK, KVHEADS, GROUP, HEAD_DIM)
    key_heads = key_window.astype(jnp.float32).reshape(window, KVHEADS, HEAD_DIM)
    value_heads = value_window.astype(jnp.float32).reshape(window, KVHEADS, HEAD_DIM)
    grad_heads = grad_block.astype(jnp.float32).reshape(BLOCK_TOK, KVHEADS, GROUP, HEAD_DIM)
    scores = jnp.einsum('qkgd,nkd->kgqn', query_heads, key_heads) * scaling
    scores = jnp.where(allowed, scores, -jnp.inf)
    highest = lax.optimization_barrier(jnp.max(scores, axis=-1, keepdims=True))
    exp_total = lax.optimization_barrier(jnp.sum(jnp.exp(scores - highest), axis=-1, keepdims=True))
    log_total = highest + jnp.log(exp_total)
    weights = jnp.exp(scores - log_total)
    weights_low = lax.optimization_barrier(weights.astype(jnp.bfloat16)).astype(jnp.float32)
    attended = jnp.einsum('kgqn,nkd->qkgd', weights_low, value_heads)
    attended = attended.reshape(BLOCK_TOK, QHEADS * HEAD_DIM).astype(jnp.bfloat16)
    attended_heads = lax.optimization_barrier(attended).astype(jnp.float32).reshape(BLOCK_TOK, KVHEADS, GROUP, HEAD_DIM)
    row_delta = jnp.einsum('qkgd,qkgd->kgq', grad_heads, attended_heads)
    grad_weights = jnp.einsum('qkgd,nkd->kgqn', grad_heads, value_heads)
    grad_scores = (weights * (grad_weights - row_delta[..., None]) * scaling).astype(jnp.bfloat16)
    grad_scores = lax.optimization_barrier(grad_scores).astype(jnp.float32)
    query_grad = jnp.einsum('kgqn,nkd->qkgd', grad_scores, key_heads)
    query_grad = query_grad.reshape(BLOCK_TOK, QHEADS * HEAD_DIM).astype(jnp.bfloat16)
    key_terms = jnp.einsum('kgqn,qkgd->nkd', grad_scores, query_heads).reshape(window, KVHEADS * HEAD_DIM)
    value_terms = jnp.einsum('kgqn,qkgd->nkd', weights_low, grad_heads).reshape(window, KVHEADS * HEAD_DIM)
    return (attended, query_grad, key_terms, value_terms)

def reference(query_rows, key_rows, value_rows, out_grad, segment_ids, home_rows):
    padding = SPAN * BLOCK_TOK
    window = (SPAN + 1) * BLOCK_TOK
    kv_width = KVHEADS * HEAD_DIM
    q_width = QHEADS * HEAD_DIM

    def one_sequence(items):
        queries, key_seq, value_seq, grad_seq, seg_seq = items
        key_pad = jnp.concatenate([jnp.zeros((padding, kv_width), jnp.bfloat16), key_seq], axis=0)
        value_pad = jnp.concatenate([jnp.zeros((padding, kv_width), jnp.bfloat16), value_seq], axis=0)
        seg_pad = jnp.concatenate([jnp.full((padding,), -1, jnp.int32), seg_seq], axis=0)

        def visit(carry, index):
            key_acc, value_acc = carry
            start = (index * BLOCK_TOK).astype(jnp.int32)
            query_block = lax.dynamic_slice_in_dim(queries, start, BLOCK_TOK, 0)
            grad_block = lax.dynamic_slice_in_dim(grad_seq, start, BLOCK_TOK, 0)
            seg_query = lax.dynamic_slice_in_dim(seg_seq, start, BLOCK_TOK, 0)
            key_window = lax.dynamic_slice_in_dim(key_pad, start, window, 0)
            value_window = lax.dynamic_slice_in_dim(value_pad, start, window, 0)
            seg_key = lax.dynamic_slice_in_dim(seg_pad, start, window, 0)
            pos_query = start + jnp.arange(BLOCK_TOK, dtype=jnp.int32)
            pos_key = start - padding + jnp.arange(window, dtype=jnp.int32)
            allowed = (seg_query[:, None] == seg_key[None, :]) & (pos_key[None, :] <= pos_query[:, None]) & (pos_key[None, :] >= 0)
            attended, query_grad, key_terms, value_terms = block_terms(query_block, key_window, value_window, grad_block, allowed)
            key_acc = lax.dynamic_update_slice_in_dim(key_acc, lax.dynamic_slice_in_dim(key_acc, start, window, 0) + key_terms, start, 0)
            value_acc = lax.dynamic_update_slice_in_dim(value_acc, lax.dynamic_slice_in_dim(value_acc, start, window, 0) + value_terms, start, 0)
            return ((key_acc, value_acc), (attended, query_grad))
        zero_acc = jnp.zeros((padding + LENGTH, kv_width), jnp.float32)
        (key_acc, value_acc), (attended, query_grad) = lax.scan(visit, (zero_acc, zero_acc), jnp.arange(BLOCKS, dtype=jnp.int32))
        return (attended.reshape(LENGTH, q_width), query_grad.reshape(LENGTH, q_width), key_acc[padding:].astype(jnp.bfloat16), value_acc[padding:].astype(jnp.bfloat16))
    attended, query_grad, key_grad, value_grad = lax.map(one_sequence, (query_rows, key_rows, value_rows, out_grad, segment_ids))
    stretch_rows = attended.reshape(SEQS, BLOCKS, STRETCHES, STRETCH * q_width).astype(jnp.float32)
    home_ids = home_rows.reshape(SEQS, BLOCKS, STRETCHES)
    positions = jnp.arange(STRETCHES, dtype=jnp.int32)
    matching = (home_ids[..., :, None] == home_ids[..., None, :]) & (positions[None, :] < positions[:, None])
    slot_index = lax.optimization_barrier(jnp.sum(matching.astype(jnp.int32), axis=-1))

    def to_home(target):
        select = ((home_ids == target)[..., None, :] & (slot_index[..., None, :] == jnp.arange(CAPACITY, dtype=jnp.int32)[:, None])).astype(jnp.float32)
        return jnp.einsum('scjk,sckx->csjx', select, stretch_rows).astype(jnp.bfloat16)
    routed = lax.map(to_home, jnp.arange(SEQS, dtype=jnp.int32))
    routed = routed.reshape(SEQS, BLOCKS, SEQS, CAPACITY, STRETCH, q_width)
    return (routed, query_grad, key_grad, value_grad)
```

```python
import functools
import math

import jax
import jax.numpy as jnp
from jax import lax
from jax.experimental import pallas as pl
from jax.experimental.pallas import tpu as pltpu
from jax.sharding import PartitionSpec as P

HEAD = 128
KV = 4
GROUP = 4
TOK = 128
WIDE = GROUP * HEAD
MESH = pl.DeviceIdType.MESH
NT = (((1,), (1,)), ((), ()))
SCALE = 1.0 / math.sqrt(HEAD)
F32 = jnp.float32
BF16 = jnp.bfloat16


def kernel(n_dp, n_ctx, q_hbm, k_hbm, v_hbm, g_hbm, seg_hbm, home_ref,
           routed, dq_hbm, dk_ref, dv_ref,
           q_s, g_s, kvx, kv1, segx, seg1, bias, sel, pk, dq_s,
           gs_out, gs_in, gz_out, gz_in, acc,
           in_sem, kv_sem, seg_send, seg_recv, f_send, f_recv, s_send, s_recv,
           a_send, a_recv, own_sem, dq_sem, gs_send, gs_recv, gz_send, gz_recv):
    dp = lax.axis_index("dp")
    ctx = lax.axis_index("ctx")
    core = lax.rem(ctx, 2)
    sib = ctx + 1 - 2 * core
    up = lax.rem(ctx + 2, n_ctx)
    down = lax.rem(ctx + n_ctx - 2, n_ctx)

    def remote(src, dst, send, recv, **where):
        return pltpu.make_async_remote_copy(
            src_ref=src, dst_ref=dst, send_sem=send, recv_sem=recv,
            device_id=where, device_id_type=MESH)

    barrier = pltpu.get_barrier_semaphore()
    pl.semaphore_signal(barrier, inc=1, device_id={"ctx": sib}, device_id_type=MESH)
    pl.semaphore_signal(barrier, inc=1, device_id={"ctx": up}, device_id_type=MESH)
    pl.semaphore_signal(barrier, inc=1, device_id={"ctx": down}, device_id_type=MESH)
    for r in range(1, n_dp):
        pl.semaphore_signal(barrier, inc=1, device_id={"dp": lax.rem(dp + r, n_dp)},
                            device_id_type=MESH)

    seg_load = pltpu.make_async_copy(seg_hbm, segx.at[0], in_sem.at[8])
    seg_load.start()
    kv_loads = []
    for h in range(KV):
        cols = pl.ds(h * HEAD, HEAD)
        kv_loads.append((
            pltpu.make_async_copy(k_hbm.at[:, cols], kvx.at[0, h, 0], kv_sem.at[h, 0]),
            pltpu.make_async_copy(v_hbm.at[:, cols], kvx.at[0, h, 1], kv_sem.at[h, 1])))
        for load in kv_loads[-1]:
            load.start()
    qg_loads = []
    for h in range(KV):
        cols = pl.ds(h * WIDE, WIDE)
        qg_loads.append(pltpu.make_async_copy(q_hbm.at[:, cols], q_s.at[h], in_sem.at[h]))
        qg_loads.append(pltpu.make_async_copy(g_hbm.at[:, cols], g_s.at[h], in_sem.at[4 + h]))
    for load in qg_loads:
        load.start()
    seg_load.wait()
    for pair in kv_loads:
        for load in pair:
            load.wait()
    pl.semaphore_wait(barrier, n_dp + 2)

    def seg_copy():
        return remote(segx.at[0], segx.at[1], seg_send.at[0], seg_recv.at[0], ctx=up)

    def seg_pass():
        return remote(segx.at[core], seg1, seg_send.at[1], seg_recv.at[1], ctx=sib)

    def fetch(h):
        return remote(kvx.at[0, h], kvx.at[1, h], f_send.at[h], f_recv.at[h], ctx=up)

    def sib_pass(h):
        return remote(kvx.at[core, h], kv1.at[h], s_send.at[h], s_recv.at[h], ctx=sib)

    def a2a(h, r):
        to = lax.rem(dp + r, n_dp)
        return remote(pk.at[h, to], routed.at[dp, :, pl.ds(pl.multiple_of(h * WIDE, WIDE), WIDE)],
                      a_send.at[h, r], a_recv.at[h, r], dp=to)

    def a2a_own(h):
        return pltpu.make_async_copy(
            pk.at[h, dp], routed.at[dp, :, pl.ds(pl.multiple_of(h * WIDE, WIDE), WIDE)],
            own_sem.at[h])

    def dq_store(h):
        return pltpu.make_async_copy(
            dq_s.at[h], dq_hbm.at[:, pl.ds(pl.multiple_of(h * WIDE, WIDE), WIDE)], dq_sem.at[h])

    def gs_copy(h):
        return remote(gs_out.at[h], gs_in.at[h], gs_send.at[h], gs_recv.at[h], ctx=sib)

    def gz_copy(h):
        return remote(gz_out.at[h], gz_in.at[h], gz_send.at[h], gz_recv.at[h], ctx=down)

    seg_copy().start()
    for h in range(KV):
        fetch(h).start()
    for load in qg_loads:
        load.wait()

    grow = lax.broadcasted_iota(jnp.int32, (16, TOK), 0)
    gcol = lax.broadcasted_iota(jnp.int32, (16, TOK), 1)
    expand = (grow == gcol // 8).astype(BF16)
    home_b = jnp.broadcast_to(home_ref[...].astype(F32), (8, 16)).astype(BF16)
    home_row = jnp.dot(home_b, expand, preferred_element_type=F32)[0:1, :]
    home_sq = jnp.broadcast_to(home_row, (TOK, TOK))
    sq_r = lax.broadcasted_iota(jnp.int32, (TOK, TOK), 0)
    sq_c = lax.broadcasted_iota(jnp.int32, (TOK, TOK), 1)
    same = (home_sq.T == home_sq) & (sq_r // 8 < sq_c // 8)
    slot_row = jnp.sum(jnp.where(same, 0.125, 0.0), axis=0, keepdims=True)
    s_r = lax.broadcasted_iota(jnp.int32, (n_dp * 16, TOK), 0)
    s_c = lax.broadcasted_iota(jnp.int32, (n_dp * 16, TOK), 1)
    pick = ((s_r // 16).astype(F32) == home_row) & ((s_r // 8 % 2).astype(F32) == slot_row)
    pick = pick & (s_r % 8 == s_c % 8)
    sel[...] = jnp.where(pick, 1.0, 0.0).astype(BF16)

    seg_copy().wait_recv()
    seg_pass().start()
    seg_pass().wait_recv()
    own_row = segx[0].astype(F32)

    def seg_equal(row):
        return jnp.broadcast_to(row.astype(F32), (TOK, TOK)).T == own_row

    low = -1e30
    bias[0:TOK, :] = jnp.where(seg_equal(segx[1]) & (ctx >= 2), 0.0, low)
    bias[TOK:2 * TOK, :] = jnp.where(seg_equal(seg1[...]) & (ctx >= 1), 0.0, low)
    bias[2 * TOK:, :] = jnp.where(seg_equal(segx[0]) & (sq_r <= sq_c), 0.0, low)

    def step(h, carry):
        fetch(h).wait_recv()
        sib_pass(h).start()
        sib_pass(h).wait_recv()
        keys = jnp.concatenate([kvx[1, h, 0], kv1[h, 0], kvx[0, h, 0]], axis=0)
        vals = jnp.concatenate([kvx[1, h, 1], kv1[h, 1], kvx[0, h, 1]], axis=0)
        qs = jnp.concatenate([q_s[h, :, g * HEAD:(g + 1) * HEAD] for g in range(GROUP)], axis=0)
        gs = jnp.concatenate([g_s[h, :, g * HEAD:(g + 1) * HEAD] for g in range(GROUP)], axis=0)
        scores = lax.dot_general(keys, qs, NT, preferred_element_type=F32)
        parts, lows = [], []
        for g in range(GROUP):
            s = scores[:, g * HEAD:(g + 1) * HEAD] * SCALE + bias[...]
            p = jnp.exp(s - jnp.max(s, axis=0, keepdims=True))
            w = p * (1.0 / jnp.sum(p, axis=0, keepdims=True))
            parts.append(w)
            lows.append(w.astype(BF16))
        low_all = jnp.concatenate(lows, axis=1)
        att = jnp.dot(vals.T, low_all, preferred_element_type=F32).astype(BF16)
        for g in range(GROUP):
            packed = lax.dot_general(sel[...], att[:, g * HEAD:(g + 1) * HEAD], NT,
                                     preferred_element_type=F32)
            pk[h, :, :, g * HEAD:(g + 1) * HEAD] = packed.astype(BF16).reshape(n_dp, 16, HEAD)
        for r in range(1, n_dp):
            a2a(h, r).start()
        a2a_own(h).start()

        gw = lax.dot_general(vals, gs, NT, preferred_element_type=F32)
        scaled = []
        for g in range(GROUP):
            gwg = gw[:, g * HEAD:(g + 1) * HEAD]
            delta = jnp.sum(lows[g].astype(F32) * gwg, axis=0, keepdims=True)
            scaled.append((parts[g] * (gwg - delta) * SCALE).astype(BF16))
        ds = jnp.concatenate(scaled, axis=1)
        dk = jnp.dot(ds, qs, preferred_element_type=F32)
        dv = jnp.dot(low_all, gs, preferred_element_type=F32)
        gs_out[h, 0] = dk[TOK:2 * TOK].astype(BF16)
        gs_out[h, 1] = dv[TOK:2 * TOK].astype(BF16)
        gs_copy(h).start()
        dqt = jnp.dot(keys.T, ds, preferred_element_type=F32)
        for g in range(GROUP):
            dq_s[h, :, g * HEAD:(g + 1) * HEAD] = dqt[:, g * HEAD:(g + 1) * HEAD].T.astype(BF16)
        dq_store(h).start()
        gs_copy(h).wait_recv()
        for i, term in ((0, dk), (1, dv)):
            other = gs_in[h, i].astype(F32)
            zero = jnp.zeros_like(other)
            gz_out[h, i] = (term[:TOK] + jnp.where(core == 1, other, zero)).astype(BF16)
            acc[h, i] = term[2 * TOK:] + jnp.where(core == 0, other, zero)
        gz_copy(h).start()
        return carry

    lax.fori_loop(0, KV, step, 0)

    for h in range(KV):
        gz_copy(h).wait_recv()
        cols = slice(h * HEAD, (h + 1) * HEAD)
        dk_ref[:, cols] = (acc[h, 0] + gz_in[h, 0].astype(F32)).astype(BF16)
        dv_ref[:, cols] = (acc[h, 1] + gz_in[h, 1].astype(F32)).astype(BF16)

    seg_copy().wait_send()
    seg_pass().wait_send()

    def drain(h, carry):
        fetch(h).wait_send()
        sib_pass(h).wait_send()
        gs_copy(h).wait_send()
        gz_copy(h).wait_send()
        dq_store(h).wait()
        a2a_own(h).wait()
        for r in range(1, n_dp):
            a2a(h, r).wait_send()
            a2a(h, r).wait_recv()
        return carry

    lax.fori_loop(0, KV, drain, 0)


def on_device(n_dp, n_ctx, query_rows, key_rows, value_rows, out_grad, segment_ids, home_rows):
    any_space = pl.BlockSpec(memory_space=pl.ANY)
    vmem = pl.BlockSpec(memory_space=pltpu.VMEM)
    dma = pltpu.SemaphoreType.DMA
    routed, dq, dk, dv = pl.pallas_call(
        functools.partial(kernel, n_dp, n_ctx),
        out_shape=(
            jax.ShapeDtypeStruct((n_dp, 16, KV * WIDE), BF16),
            jax.ShapeDtypeStruct((TOK, KV * WIDE), BF16),
            jax.ShapeDtypeStruct((TOK, KV * HEAD), BF16),
            jax.ShapeDtypeStruct((TOK, KV * HEAD), BF16),
        ),
        in_specs=[any_space] * 5 + [vmem],
        out_specs=(any_space, any_space, vmem, vmem),
        scratch_shapes=[
            pltpu.VMEM((KV, TOK, WIDE), BF16),
            pltpu.VMEM((KV, TOK, WIDE), BF16),
            pltpu.VMEM((2, KV, 2, TOK, HEAD), BF16),
            pltpu.VMEM((KV, 2, TOK, HEAD), BF16),
            pltpu.VMEM((2, 1, TOK), jnp.int32),
            pltpu.VMEM((1, TOK), jnp.int32),
            pltpu.VMEM((3 * TOK, TOK), F32),
            pltpu.VMEM((n_dp * 16, TOK), BF16),
            pltpu.VMEM((KV, n_dp, 16, WIDE), BF16),
            pltpu.VMEM((KV, TOK, WIDE), BF16),
            pltpu.VMEM((KV, 2, TOK, HEAD), BF16),
            pltpu.VMEM((KV, 2, TOK, HEAD), BF16),
            pltpu.VMEM((KV, 2, TOK, HEAD), BF16),
            pltpu.VMEM((KV, 2, TOK, HEAD), BF16),
            pltpu.VMEM((KV, 2, TOK, HEAD), F32),
            dma((9,)), dma((KV, 2)), dma((2,)), dma((2,)),
            dma((KV,)), dma((KV,)), dma((KV,)), dma((KV,)),
            dma((KV, n_dp)), dma((KV, n_dp)), dma((KV,)), dma((KV,)),
            dma((KV,)), dma((KV,)), dma((KV,)), dma((KV,)),
        ],
        compiler_params=pltpu.CompilerParams(collective_id=0, has_side_effects=True),
        name="fused_attention",
    )(query_rows[0], key_rows[0], value_rows[0], out_grad[0], segment_ids, home_rows)
    return (routed.reshape(1, 1, n_dp, 2, 8, KV * WIDE), dq[None], dk[None], dv[None])


def solution(mesh):
    n_dp, n_ctx = mesh.shape["dp"], mesh.shape["ctx"]
    rows = P("dp", "ctx", None)
    return jax.shard_map(
        functools.partial(on_device, n_dp, n_ctx),
        mesh=mesh,
        in_specs=(rows, rows, rows, rows, P("dp", "ctx"), P("dp", "ctx")),
        out_specs=(P("dp", "ctx", None, None, None, None), rows, rows, rows),
        check_vma=False,
    )
```

```python
import functools
import math

import jax
import jax.numpy as jnp
from jax import lax
from jax.experimental import pallas as pl
from jax.experimental.pallas import tpu as pltpu
from jax.sharding import PartitionSpec as P

HEAD = 128
KV = 4
GROUP = 4
TOK = 128
WIDE = GROUP * HEAD
MESH = pl.DeviceIdType.MESH
NT = (((1,), (1,)), ((), ()))
SCALE = 1.0 / math.sqrt(HEAD)
F32 = jnp.float32
BF16 = jnp.bfloat16


def kernel(n_dp, n_ctx, q_hbm, k_hbm, v_hbm, g_hbm, seg_hbm, home_ref,
           routed, dq_hbm, dk_ref, dv_ref,
           q_s, g_s, kvx, kv1, segx, seg1, bias, sel, pk, dq_s,
           gs_out, gs_in, gz_out, gz_in, acc,
           in_sem, kv_sem, seg_send, seg_recv, f_send, f_recv, s_send, s_recv,
           a_send, a_recv, own_sem, dq_sem, gs_send, gs_recv, gz_send, gz_recv, met):
    dp = lax.axis_index("dp")
    ctx = lax.axis_index("ctx")
    core = lax.rem(ctx, 2)
    first = lax.rem(ctx // 2, 3)
    ahead = jnp.where(lax.rem(dp, 4) < 2, 2, 4)
    sib = ctx + 1 - 2 * core
    up = lax.rem(ctx + 2, n_ctx)
    down = lax.rem(ctx + n_ctx - 2, n_ctx)

    def remote(src, dst, send, recv, **where):
        return pltpu.make_async_remote_copy(
            src_ref=src, dst_ref=dst, send_sem=send, recv_sem=recv,
            device_id=where, device_id_type=MESH)

    barrier = pltpu.get_barrier_semaphore()
    pl.semaphore_signal(barrier, inc=1, device_id={"ctx": sib}, device_id_type=MESH)
    pl.semaphore_signal(barrier, inc=1, device_id={"ctx": down}, device_id_type=MESH)
    partners = []
    for bit in range(n_dp.bit_length() - 1):
        partners.append(dp + (1 << bit) - (2 << bit) * lax.rem(dp // (1 << bit), 2))
        pl.semaphore_signal(barrier, inc=1, device_id={"dp": partners[-1]}, device_id_type=MESH)

    seg_load = pltpu.make_async_copy(seg_hbm, segx.at[0], in_sem.at[8])
    seg_load.start()
    kv_loads = []
    for h in range(KV):
        cols = pl.ds(h * HEAD, HEAD)
        kv_loads.append((
            pltpu.make_async_copy(k_hbm.at[:, cols], kvx.at[0, h, 0], kv_sem.at[h, 0]),
            pltpu.make_async_copy(v_hbm.at[:, cols], kvx.at[0, h, 1], kv_sem.at[h, 1])))
        for load in kv_loads[-1]:
            load.start()
    qg_loads = []
    for h in range(KV):
        cols = pl.ds(h * WIDE, WIDE)
        qg_loads.append(pltpu.make_async_copy(q_hbm.at[:, cols], q_s.at[h], in_sem.at[h]))
        qg_loads.append(pltpu.make_async_copy(g_hbm.at[:, cols], g_s.at[h], in_sem.at[4 + h]))
    for load in qg_loads:
        load.start()
    seg_load.wait()
    for pair in kv_loads:
        for load in pair:
            load.wait()
    pl.semaphore_wait(barrier, 2 + len(partners))

    def seg_copy():
        return remote(segx.at[0], segx.at[1], seg_send.at[0], seg_recv.at[0], ctx=up)

    def seg_pass():
        return remote(segx.at[core], seg1, seg_send.at[1], seg_recv.at[1], ctx=sib)

    def fetch(h):
        return remote(kvx.at[0, h], kvx.at[1, h], f_send.at[h], f_recv.at[h], ctx=up)

    def sib_pass(h):
        return remote(kvx.at[core, h], kv1.at[h], s_send.at[h], s_recv.at[h], ctx=sib)

    def a2a(h, r):
        to = lax.rem(dp + r, n_dp)
        return remote(pk.at[h, to], routed.at[dp, :, pl.ds(pl.multiple_of(h * WIDE, WIDE), WIDE)],
                      a_send.at[h, r], a_recv.at[h, r], dp=to)

    def a2a_own(h):
        return pltpu.make_async_copy(
            pk.at[h, dp], routed.at[dp, :, pl.ds(pl.multiple_of(h * WIDE, WIDE), WIDE)],
            own_sem.at[h])

    def dq_store(h):
        return pltpu.make_async_copy(
            dq_s.at[h], dq_hbm.at[:, pl.ds(pl.multiple_of(h * WIDE, WIDE), WIDE)], dq_sem.at[h])

    def gs_copy(h):
        return remote(gs_out.at[h], gs_in.at[h], gs_send.at[h], gs_recv.at[h], ctx=sib)

    def gz_copy(h):
        return remote(gz_out.at[h], gz_in.at[h], gz_send.at[h], gz_recv.at[h], ctx=down)

    seg_copy().start()
    for h in range(KV):
        @pl.when(h < ahead)
        def _(h=h):
            fetch(h).start()
    for i, partner in enumerate(partners):
        pl.semaphore_signal(met.at[i], inc=1, device_id={"dp": partner}, device_id_type=MESH)
        pl.semaphore_wait(met.at[i], 1)
    for load in qg_loads:
        load.wait()

    grow = lax.broadcasted_iota(jnp.int32, (16, TOK), 0)
    gcol = lax.broadcasted_iota(jnp.int32, (16, TOK), 1)
    expand = (grow == gcol // 8).astype(BF16)
    home_b = jnp.broadcast_to(home_ref[...].astype(F32), (8, 16)).astype(BF16)
    home_row = jnp.dot(home_b, expand, preferred_element_type=F32)[0:1, :]
    home_sq = jnp.broadcast_to(home_row, (TOK, TOK))
    sq_r = lax.broadcasted_iota(jnp.int32, (TOK, TOK), 0)
    sq_c = lax.broadcasted_iota(jnp.int32, (TOK, TOK), 1)
    same = (home_sq.T == home_sq) & (sq_r // 8 < sq_c // 8)
    slot_row = jnp.sum(jnp.where(same, 0.125, 0.0), axis=0, keepdims=True)
    s_r = lax.broadcasted_iota(jnp.int32, (n_dp * 16, TOK), 0)
    s_c = lax.broadcasted_iota(jnp.int32, (n_dp * 16, TOK), 1)
    pick = ((s_r // 16).astype(F32) == home_row) & ((s_r // 8 % 2).astype(F32) == slot_row)
    pick = pick & (s_r % 8 == s_c % 8)
    sel[...] = jnp.where(pick, 1.0, 0.0).astype(BF16)

    seg_copy().wait_recv()
    seg_pass().start()
    fetch(0).wait_recv()
    sib_pass(0).start()

    for h in range(1, KV):
        @pl.when(h >= ahead)
        def _(h=h):
            fetch(h).start()

    seg_pass().wait_recv()
    own_row = segx[0].astype(F32)

    def seg_equal(row):
        return jnp.broadcast_to(row.astype(F32), (TOK, TOK)).T == own_row

    low = -1e30
    bias[0:TOK, :] = jnp.where(seg_equal(segx[1]) & (ctx >= 2), 0.0, low)
    bias[TOK:2 * TOK, :] = jnp.where(seg_equal(seg1[...]) & (ctx >= 1), 0.0, low)
    bias[2 * TOK:, :] = jnp.where(seg_equal(segx[0]) & (sq_r <= sq_c), 0.0, low)

    def step(h, carry):
        sib_pass(h).wait_recv()
        keys = jnp.concatenate([kvx[1, h, 0], kv1[h, 0], kvx[0, h, 0]], axis=0)
        vals = jnp.concatenate([kvx[1, h, 1], kv1[h, 1], kvx[0, h, 1]], axis=0)
        qs = jnp.concatenate([q_s[h, :, g * HEAD:(g + 1) * HEAD] for g in range(GROUP)], axis=0)
        gs = jnp.concatenate([g_s[h, :, g * HEAD:(g + 1) * HEAD] for g in range(GROUP)], axis=0)
        scores = lax.dot_general(keys, qs, NT, preferred_element_type=F32)
        parts, lows = [], []
        for g in range(GROUP):
            s = scores[:, g * HEAD:(g + 1) * HEAD] * SCALE + bias[...]
            p = jnp.exp(s - jnp.max(s, axis=0, keepdims=True))
            w = p * (1.0 / jnp.sum(p, axis=0, keepdims=True))
            parts.append(w)
            lows.append(w.astype(BF16))
        low_all = jnp.concatenate(lows, axis=1)
        att = jnp.dot(vals.T, low_all, preferred_element_type=F32).astype(BF16)
        for g in range(GROUP):
            packed = lax.dot_general(sel[...], att[:, g * HEAD:(g + 1) * HEAD], NT,
                                     preferred_element_type=F32)
            pk[h, :, :, g * HEAD:(g + 1) * HEAD] = packed.astype(BF16).reshape(n_dp, 16, HEAD)
        for r in range(1, n_dp):
            a2a(h, r).start()
        a2a_own(h).start()

        gw = lax.dot_general(vals, gs, NT, preferred_element_type=F32)
        scaled = []
        for g in range(GROUP):
            gwg = gw[:, g * HEAD:(g + 1) * HEAD]
            delta = jnp.sum(lows[g].astype(F32) * gwg, axis=0, keepdims=True)
            scaled.append((parts[g] * (gwg - delta) * SCALE).astype(BF16))
        ds = jnp.concatenate(scaled, axis=1)
        dk = jnp.dot(ds, qs, preferred_element_type=F32)
        dv = jnp.dot(low_all, gs, preferred_element_type=F32)
        gs_out[h, 0] = dk[TOK:2 * TOK].astype(BF16)
        gs_out[h, 1] = dv[TOK:2 * TOK].astype(BF16)
        gs_copy(h).start()
        dqt = jnp.dot(keys.T, ds, preferred_element_type=F32)
        for g in range(GROUP):
            dq_s[h, :, g * HEAD:(g + 1) * HEAD] = dqt[:, g * HEAD:(g + 1) * HEAD].T.astype(BF16)
        dq_store(h).start()

        @pl.when(h < KV - 1)
        def _():
            fetch(h + 1).wait_recv()
            sib_pass(h + 1).start()

        gs_copy(h).wait_recv()
        for i, term in ((0, dk), (1, dv)):
            other = gs_in[h, i].astype(F32)
            zero = jnp.zeros_like(other)
            gz_out[h, i] = (term[:TOK] + jnp.where(core == 1, other, zero)).astype(BF16)
            acc[h, i] = term[2 * TOK:] + jnp.where(core == 0, other, zero)

        @pl.when(first != 0)
        def _():
            gz_copy(h).start()

        return carry

    lax.fori_loop(0, KV, step, 0)

    @pl.when(first == 0)
    def _():
        for h in range(KV):
            gz_copy(h).start()


    for h in range(KV):
        gz_copy(h).wait_recv()
        cols = slice(h * HEAD, (h + 1) * HEAD)
        dk_ref[:, cols] = (acc[h, 0] + gz_in[h, 0].astype(F32)).astype(BF16)
        dv_ref[:, cols] = (acc[h, 1] + gz_in[h, 1].astype(F32)).astype(BF16)

    seg_copy().wait_send()
    seg_pass().wait_send()

    def drain(h, carry):
        fetch(h).wait_send()
        sib_pass(h).wait_send()
        gs_copy(h).wait_send()
        gz_copy(h).wait_send()
        dq_store(h).wait()
        a2a_own(h).wait()
        for r in range(1, n_dp):
            a2a(h, r).wait_send()
            a2a(h, r).wait_recv()
        return carry

    lax.fori_loop(0, KV, drain, 0)


def settle(*refs):
    done = refs[8]
    copies = [pltpu.make_async_copy(refs[i], refs[4 + i], done.at[i]) for i in range(4)]
    for copy in copies:
        copy.start()
    for copy in copies:
        copy.wait()


def on_device(n_dp, n_ctx, query_rows, key_rows, value_rows, out_grad, segment_ids, home_rows):
    hbm = pl.BlockSpec(memory_space=pltpu.HBM)
    any_space = pl.BlockSpec(memory_space=pl.ANY)
    vmem = pl.BlockSpec(memory_space=pltpu.VMEM)
    dma = pltpu.SemaphoreType.DMA
    routed, dq, dk, dv = pl.pallas_call(
        functools.partial(kernel, n_dp, n_ctx),
        out_shape=(
            jax.ShapeDtypeStruct((n_dp, 16, KV * WIDE), BF16),
            jax.ShapeDtypeStruct((TOK, KV * WIDE), BF16),
            jax.ShapeDtypeStruct((TOK, KV * HEAD), BF16),
            jax.ShapeDtypeStruct((TOK, KV * HEAD), BF16),
        ),
        in_specs=[hbm] * 5 + [vmem],
        out_specs=(any_space, any_space, vmem, vmem),
        scratch_shapes=[
            pltpu.VMEM((KV, TOK, WIDE), BF16),
            pltpu.VMEM((KV, TOK, WIDE), BF16),
            pltpu.VMEM((2, KV, 2, TOK, HEAD), BF16),
            pltpu.VMEM((KV, 2, TOK, HEAD), BF16),
            pltpu.VMEM((2, 1, TOK), jnp.int32),
            pltpu.VMEM((1, TOK), jnp.int32),
            pltpu.VMEM((3 * TOK, TOK), F32),
            pltpu.VMEM((n_dp * 16, TOK), BF16),
            pltpu.VMEM((KV, n_dp, 16, WIDE), BF16),
            pltpu.VMEM((KV, TOK, WIDE), BF16),
            pltpu.VMEM((KV, 2, TOK, HEAD), BF16),
            pltpu.VMEM((KV, 2, TOK, HEAD), BF16),
            pltpu.VMEM((KV, 2, TOK, HEAD), BF16),
            pltpu.VMEM((KV, 2, TOK, HEAD), BF16),
            pltpu.VMEM((KV, 2, TOK, HEAD), F32),
            dma((9,)), dma((KV, 2)), dma((2,)), dma((2,)),
            dma((KV,)), dma((KV,)), dma((KV,)), dma((KV,)),
            dma((KV, n_dp)), dma((KV, n_dp)), dma((KV,)), dma((KV,)),
            dma((KV,)), dma((KV,)), dma((KV,)), dma((KV,)),
            pltpu.SemaphoreType.REGULAR((4,)),
        ],
        compiler_params=pltpu.CompilerParams(collective_id=0, has_side_effects=True,
                                             vmem_limit_bytes=24 * 1024 * 1024),
        name="fused_attention",
    )(query_rows[0], key_rows[0], value_rows[0], out_grad[0], segment_ids, home_rows)
    routed, dq, dk, dv = pl.pallas_call(
        settle,
        out_shape=tuple(jax.ShapeDtypeStruct(a.shape, a.dtype) for a in (routed, dq, dk, dv)),
        in_specs=[any_space] * 4,
        out_specs=(hbm,) * 4,
        scratch_shapes=[dma((4,))],
        compiler_params=pltpu.CompilerParams(vmem_limit_bytes=1024 * 1024),
        name="settle",
    )(routed, dq, dk, dv)
    return (routed.reshape(1, 1, n_dp, 2, 8, KV * WIDE), dq[None], dk[None], dv[None])


def solution(mesh):
    n_dp, n_ctx = mesh.shape["dp"], mesh.shape["ctx"]
    rows = P("dp", "ctx", None)
    return jax.shard_map(
        functools.partial(on_device, n_dp, n_ctx),
        mesh=mesh,
        in_specs=(rows, rows, rows, rows, P("dp", "ctx"), P("dp", "ctx")),
        out_specs=(P("dp", "ctx", None, None, None, None), rows, rows, rows),
        check_vma=False,
    )
```

```python
import functools
import math

import jax
import jax.numpy as jnp
from jax import lax
from jax.experimental import pallas as pl
from jax.experimental.pallas import tpu as pltpu
from jax.sharding import PartitionSpec as P

HEAD = 128
KV = 4
GROUP = 4
TOK = 128
WIDE = GROUP * HEAD
MESH = pl.DeviceIdType.MESH
NT = (((1,), (1,)), ((), ()))
SCALE = 1.0 / math.sqrt(HEAD)
F32 = jnp.float32
BF16 = jnp.bfloat16


def kernel(n_dp, n_ctx, q_hbm, k_hbm, v_hbm, g_hbm, seg_hbm, home_hbm,
           routed, dq_hbm, dk_ref, dv_ref,
           home_s, q_s, g_s, kvx, kv1, segx, seg1, bias, sel, pk, dq_s,
           gs_out, gs_in, gz_out, gz_in, acc,
           in_sem, kv_sem, seg_send, seg_recv, f_send, f_recv, s_send, s_recv,
           a_send, a_recv, own_sem, dq_sem, gs_send, gs_recv, gz_send, gz_recv, met):
    dp = lax.axis_index("dp")
    ctx = lax.axis_index("ctx")
    core = lax.rem(ctx, 2)
    first = jnp.where(lax.rem(dp, 4) < 2, 1, lax.rem(ctx // 2, 3))
    ahead = jnp.where(lax.rem(dp, 4) < 2, 2 - lax.rem(dp, 4), 4)
    sib = ctx + 1 - 2 * core
    up = lax.rem(ctx + 2, n_ctx)
    down = lax.rem(ctx + n_ctx - 2, n_ctx)

    def remote(src, dst, send, recv, **where):
        return pltpu.make_async_remote_copy(
            src_ref=src, dst_ref=dst, send_sem=send, recv_sem=recv,
            device_id=where, device_id_type=MESH)

    barrier = pltpu.get_barrier_semaphore()
    pl.semaphore_signal(barrier, inc=1, device_id={"ctx": sib}, device_id_type=MESH)
    pl.semaphore_signal(barrier, inc=1, device_id={"ctx": down}, device_id_type=MESH)
    partners = []
    for bit in range(n_dp.bit_length() - 1):
        partners.append(dp + (1 << bit) - (2 << bit) * lax.rem(dp // (1 << bit), 2))
        pl.semaphore_signal(barrier, inc=1, device_id={"dp": partners[-1]}, device_id_type=MESH)

    seg_load = pltpu.make_async_copy(seg_hbm, segx.at[0], in_sem.at[8])
    seg_load.start()
    home_load = pltpu.make_async_copy(home_hbm, home_s, in_sem.at[9])
    home_load.start()
    kv_loads = []
    for h in range(KV):
        cols = pl.ds(h * HEAD, HEAD)
        kv_loads.append((
            pltpu.make_async_copy(k_hbm.at[:, cols], kvx.at[0, h, 0], kv_sem.at[h, 0]),
            pltpu.make_async_copy(v_hbm.at[:, cols], kvx.at[0, h, 1], kv_sem.at[h, 1])))
        for load in kv_loads[-1]:
            load.start()
    qg_loads = []
    for h in range(KV):
        cols = pl.ds(h * WIDE, WIDE)
        qg_loads.append(pltpu.make_async_copy(q_hbm.at[:, cols], q_s.at[h], in_sem.at[h]))
        qg_loads.append(pltpu.make_async_copy(g_hbm.at[:, cols], g_s.at[h], in_sem.at[4 + h]))
    for load in qg_loads:
        load.start()
    seg_load.wait()
    home_load.wait()
    for pair in kv_loads:
        for load in pair:
            load.wait()
    pl.semaphore_wait(barrier, 2 + len(partners))

    def seg_copy():
        return remote(segx.at[0], segx.at[1], seg_send.at[0], seg_recv.at[0], ctx=up)

    def seg_pass():
        return remote(segx.at[core], seg1, seg_send.at[1], seg_recv.at[1], ctx=sib)

    def fetch(h):
        return remote(kvx.at[0, h], kvx.at[1, h], f_send.at[h], f_recv.at[h], ctx=up)

    def sib_pass(h):
        return remote(kvx.at[core, h], kv1.at[h], s_send.at[h], s_recv.at[h], ctx=sib)

    def a2a(h, r):
        to = lax.rem(dp + r, n_dp)
        return remote(pk.at[h, to], routed.at[dp, :, pl.ds(pl.multiple_of(h * WIDE, WIDE), WIDE)],
                      a_send.at[h, r], a_recv.at[h, r], dp=to)

    def a2a_own(h):
        return pltpu.make_async_copy(
            pk.at[h, dp], routed.at[dp, :, pl.ds(pl.multiple_of(h * WIDE, WIDE), WIDE)],
            own_sem.at[h])

    def dq_store(h):
        return pltpu.make_async_copy(
            dq_s.at[h], dq_hbm.at[:, pl.ds(pl.multiple_of(h * WIDE, WIDE), WIDE)], dq_sem.at[h])

    def gs_copy(h):
        return remote(gs_out.at[h], gs_in.at[h], gs_send.at[h], gs_recv.at[h], ctx=sib)

    def gz_copy(h):
        return remote(gz_out.at[h], gz_in.at[h], gz_send.at[h], gz_recv.at[h], ctx=down)

    seg_copy().start()
    for h in range(KV):
        @pl.when(h < ahead)
        def _(h=h):
            fetch(h).start()
    for i, partner in enumerate(partners):
        pl.semaphore_signal(met.at[i], inc=1, device_id={"dp": partner}, device_id_type=MESH)
        pl.semaphore_wait(met.at[i], 1)
    for load in qg_loads:
        load.wait()

    grow = lax.broadcasted_iota(jnp.int32, (16, TOK), 0)
    gcol = lax.broadcasted_iota(jnp.int32, (16, TOK), 1)
    expand = (grow == gcol // 8).astype(BF16)
    home_b = jnp.broadcast_to(home_s[...].astype(F32), (8, 16)).astype(BF16)
    home_row = jnp.dot(home_b, expand, preferred_element_type=F32)[0:1, :]
    home_sq = jnp.broadcast_to(home_row, (TOK, TOK))
    sq_r = lax.broadcasted_iota(jnp.int32, (TOK, TOK), 0)
    sq_c = lax.broadcasted_iota(jnp.int32, (TOK, TOK), 1)
    same = (home_sq.T == home_sq) & (sq_r // 8 < sq_c // 8)
    slot_row = jnp.sum(jnp.where(same, 0.125, 0.0), axis=0, keepdims=True)
    s_r = lax.broadcasted_iota(jnp.int32, (n_dp * 16, TOK), 0)
    s_c = lax.broadcasted_iota(jnp.int32, (n_dp * 16, TOK), 1)
    pick = ((s_r // 16).astype(F32) == home_row) & ((s_r // 8 % 2).astype(F32) == slot_row)
    pick = pick & (s_r % 8 == s_c % 8)
    sel[...] = jnp.where(pick, 1.0, 0.0).astype(BF16)

    seg_copy().wait_recv()
    seg_pass().start()
    fetch(0).wait_recv()
    sib_pass(0).start()

    for h in range(1, KV):
        @pl.when(h >= ahead)
        def _(h=h):
            fetch(h).start()

    seg_pass().wait_recv()
    own_row = segx[0].astype(F32)

    def seg_equal(row):
        return jnp.broadcast_to(row.astype(F32), (TOK, TOK)).T == own_row

    low = -1e30
    bias[0:TOK, :] = jnp.where(seg_equal(segx[1]) & (ctx >= 2), 0.0, low)
    bias[TOK:2 * TOK, :] = jnp.where(seg_equal(seg1[...]) & (ctx >= 1), 0.0, low)
    bias[2 * TOK:, :] = jnp.where(seg_equal(segx[0]) & (sq_r <= sq_c), 0.0, low)

    def step(h, carry):
        sib_pass(h).wait_recv()
        keys = jnp.concatenate([kvx[1, h, 0], kv1[h, 0], kvx[0, h, 0]], axis=0)
        vals = jnp.concatenate([kvx[1, h, 1], kv1[h, 1], kvx[0, h, 1]], axis=0)
        qs = jnp.concatenate([q_s[h, :, g * HEAD:(g + 1) * HEAD] for g in range(GROUP)], axis=0)
        gs = jnp.concatenate([g_s[h, :, g * HEAD:(g + 1) * HEAD] for g in range(GROUP)], axis=0)
        scores = lax.dot_general(keys, qs, NT, preferred_element_type=F32)
        parts, lows = [], []
        for g in range(GROUP):
            s = scores[:, g * HEAD:(g + 1) * HEAD] * SCALE + bias[...]
            p = jnp.exp(s - jnp.max(s, axis=0, keepdims=True))
            w = p * (1.0 / jnp.sum(p, axis=0, keepdims=True))
            parts.append(w)
            lows.append(w.astype(BF16))
        low_all = jnp.concatenate(lows, axis=1)
        att = jnp.dot(vals.T, low_all, preferred_element_type=F32).astype(BF16)
        for g in range(GROUP):
            packed = lax.dot_general(sel[...], att[:, g * HEAD:(g + 1) * HEAD], NT,
                                     preferred_element_type=F32)
            pk[h, :, :, g * HEAD:(g + 1) * HEAD] = packed.astype(BF16).reshape(n_dp, 16, HEAD)
        for r in range(1, n_dp):
            a2a(h, r).start()
        a2a_own(h).start()

        gw = lax.dot_general(vals, gs, NT, preferred_element_type=F32)
        scaled = []
        for g in range(GROUP):
            gwg = gw[:, g * HEAD:(g + 1) * HEAD]
            delta = jnp.sum(lows[g].astype(F32) * gwg, axis=0, keepdims=True)
            scaled.append((parts[g] * (gwg - delta) * SCALE).astype(BF16))
        ds = jnp.concatenate(scaled, axis=1)
        dk = jnp.dot(ds, qs, preferred_element_type=F32)
        dv = jnp.dot(low_all, gs, preferred_element_type=F32)
        gs_out[h, 0] = dk[TOK:2 * TOK].astype(BF16)
        gs_out[h, 1] = dv[TOK:2 * TOK].astype(BF16)
        gs_copy(h).start()
        dqt = jnp.dot(keys.T, ds, preferred_element_type=F32)
        for g in range(GROUP):
            dq_s[h, :, g * HEAD:(g + 1) * HEAD] = dqt[:, g * HEAD:(g + 1) * HEAD].T.astype(BF16)
        dq_store(h).start()

        @pl.when(h < KV - 1)
        def _():
            fetch(h + 1).wait_recv()
            sib_pass(h + 1).start()

        gs_copy(h).wait_recv()
        for i, term in ((0, dk), (1, dv)):
            other = gs_in[h, i].astype(F32)
            zero = jnp.zeros_like(other)
            gz_out[h, i] = (term[:TOK] + jnp.where(core == 1, other, zero)).astype(BF16)
            acc[h, i] = term[2 * TOK:] + jnp.where(core == 0, other, zero)

        @pl.when(first != 0)
        def _():
            gz_copy(h).start()

        return carry

    lax.fori_loop(0, KV, step, 0)

    @pl.when(first == 0)
    def _():
        for h in range(KV):
            gz_copy(h).start()


    for h in range(KV):
        gz_copy(h).wait_recv()
        cols = slice(h * HEAD, (h + 1) * HEAD)
        dk_ref[:, cols] = (acc[h, 0] + gz_in[h, 0].astype(F32)).astype(BF16)
        dv_ref[:, cols] = (acc[h, 1] + gz_in[h, 1].astype(F32)).astype(BF16)

    seg_copy().wait_send()
    seg_pass().wait_send()

    def drain(h, carry):
        fetch(h).wait_send()
        sib_pass(h).wait_send()
        gs_copy(h).wait_send()
        gz_copy(h).wait_send()
        dq_store(h).wait()
        a2a_own(h).wait()
        for r in range(1, n_dp):
            a2a(h, r).wait_send()
            a2a(h, r).wait_recv()
        return carry

    lax.fori_loop(0, KV, drain, 0)


def settle(*refs):
    done = refs[8]
    copies = [pltpu.make_async_copy(refs[i], refs[4 + i], done.at[i]) for i in range(4)]
    for copy in copies:
        copy.start()
    for copy in copies:
        copy.wait()


def on_device(n_dp, n_ctx, query_rows, key_rows, value_rows, out_grad, segment_ids, home_rows):
    hbm = pl.BlockSpec(memory_space=pltpu.HBM)
    any_space = pl.BlockSpec(memory_space=pl.ANY)
    vmem = pl.BlockSpec(memory_space=pltpu.VMEM)
    dma = pltpu.SemaphoreType.DMA
    routed, dq, dk, dv = pl.pallas_call(
        functools.partial(kernel, n_dp, n_ctx),
        out_shape=(
            jax.ShapeDtypeStruct((n_dp, 16, KV * WIDE), BF16),
            jax.ShapeDtypeStruct((TOK, KV * WIDE), BF16),
            jax.ShapeDtypeStruct((TOK, KV * HEAD), BF16),
            jax.ShapeDtypeStruct((TOK, KV * HEAD), BF16),
        ),
        in_specs=[hbm] * 6,
        out_specs=(any_space, any_space, vmem, vmem),
        scratch_shapes=[
            pltpu.VMEM((1, 16), jnp.int32),
            pltpu.VMEM((KV, TOK, WIDE), BF16),
            pltpu.VMEM((KV, TOK, WIDE), BF16),
            pltpu.VMEM((2, KV, 2, TOK, HEAD), BF16),
            pltpu.VMEM((KV, 2, TOK, HEAD), BF16),
            pltpu.VMEM((2, 1, TOK), jnp.int32),
            pltpu.VMEM((1, TOK), jnp.int32),
            pltpu.VMEM((3 * TOK, TOK), F32),
            pltpu.VMEM((n_dp * 16, TOK), BF16),
            pltpu.VMEM((KV, n_dp, 16, WIDE), BF16),
            pltpu.VMEM((KV, TOK, WIDE), BF16),
            pltpu.VMEM((KV, 2, TOK, HEAD), BF16),
            pltpu.VMEM((KV, 2, TOK, HEAD), BF16),
            pltpu.VMEM((KV, 2, TOK, HEAD), BF16),
            pltpu.VMEM((KV, 2, TOK, HEAD), BF16),
            pltpu.VMEM((KV, 2, TOK, HEAD), F32),
            dma((10,)), dma((KV, 2)), dma((2,)), dma((2,)),
            dma((KV,)), dma((KV,)), dma((KV,)), dma((KV,)),
            dma((KV, n_dp)), dma((KV, n_dp)), dma((KV,)), dma((KV,)),
            dma((KV,)), dma((KV,)), dma((KV,)), dma((KV,)),
            pltpu.SemaphoreType.REGULAR((4,)),
        ],
        compiler_params=pltpu.CompilerParams(collective_id=0, has_side_effects=True,
                                             vmem_limit_bytes=24 * 1024 * 1024),
        name="fused_attention",
    )(*(pltpu.with_memory_space_constraint(a, pltpu.HBM) for a in (
        query_rows[0], key_rows[0], value_rows[0], out_grad[0], segment_ids, home_rows)))
    routed, dq, dk, dv = pl.pallas_call(
        settle,
        out_shape=tuple(jax.ShapeDtypeStruct(a.shape, a.dtype) for a in (routed, dq, dk, dv)),
        in_specs=[any_space] * 4,
        out_specs=(hbm,) * 4,
        scratch_shapes=[dma((4,))],
        compiler_params=pltpu.CompilerParams(vmem_limit_bytes=1024 * 1024),
        name="settle",
    )(routed, dq, dk, dv)
    return (routed.reshape(1, 1, n_dp, 2, 8, KV * WIDE), dq[None], dk[None], dv[None])


def solution(mesh):
    n_dp, n_ctx = mesh.shape["dp"], mesh.shape["ctx"]
    rows = P("dp", "ctx", None)
    return jax.shard_map(
        functools.partial(on_device, n_dp, n_ctx),
        mesh=mesh,
        in_specs=(rows, rows, rows, rows, P("dp", "ctx"), P("dp", "ctx")),
        out_specs=(P("dp", "ctx", None, None, None, None), rows, rows, rows),
        check_vma=False,
    )
```
